512 devices in a mesh: dp: 64 (over z, y), sub: 8 (over x, core).
Axes of the slice: x: 4, y: 4, z: 16, core: 2. Of those that a mesh axis runs over, the one named last changes fastest.
Arguments:
- embeddings: bfloat16 [524288, 1024], P(('dp', 'sub')), may hold values from -6 to 6
- cluster_of: int32 [524288], P(('dp', 'sub')), may hold values from 0 to 1087, as said below
Outputs:
- density: float32 [524288], P(('dp', 'sub'))
The draws below stay inside these ranges and needn't reach their ends.
Inputs may be any that keep to these rules, and one draw needn't show every extreme that they name: `cluster_of`: A cluster c < 2 * 512 is held whole by the device of dp index (c // 2) // 8 and sub index (c // 2) % 8; a cluster c >= 2 * 512 is spread over the sub devices of dp index (c - 2 * 512). Of one device's rows exactly 896 lie in whole-held clusters and 128 in spread ones. At most 3 of one device's rows lie in the whole-held clusters of one device; one device gets exactly 3 such rows from every device. At most 4 of one device's rows lie in the spread clusters of one dp index; one dp index gets exactly 4 such rows from every device.
All inputs are finite; a program needn't handle non-finite values.
Results may differ from the reference program's by a relative error of at most 0.0005.
The reference program's roundings to bfloat16 on the way count: a program that leaves them out, or rounds other values in their place, can miss the bound.
Values may be sent and summed in bfloat16 or wider, within the bound.
A program may use at most 64 MiB of HBM per device.

```python
import jax
import jax.numpy as jnp
from jax import lax

D = 1024
ROWS_DEV = 1024
SC = 2
LC = 1
RL = 128
RS = 896
CAPS = 3
CAPL = 4
SS = 1536
LS = 256
ROWS = 524288
N_DP = 64
N_SUB = 8
DEVICES = 512


def draw_cluster_of(key, part):
    full_device = jax.random.randint(jax.random.fold_in(key, 12), (), 0, DEVICES)
    full_owner = jax.random.randint(jax.random.fold_in(key, 13), (), 0, N_DP)
    block_keys = jax.random.split(jax.random.fold_in(key, 14), DEVICES)

    def one_block(block_key):
        first, second, third, fourth, fifth, sixth = jax.random.split(block_key, 6)
        whole_slots = DEVICES * CAPS
        slot_ids = jnp.arange(whole_slots, dtype=jnp.int32)
        scores = jax.random.randint(first, (whole_slots,), 0, 1 << 20) * whole_slots + slot_ids
        scores = jnp.where(slot_ids // CAPS == full_device, slot_ids - whole_slots, scores)
        picked = jnp.argsort(scores, stable=True)[:RS].astype(jnp.int32)
        holder = picked // CAPS
        local_pick = jnp.minimum(jax.random.randint(second, (RS,), 0, SC), jax.random.randint(third, (RS,), 0, SC))
        whole_rows = holder * SC + local_pick
        spread_slots = N_DP * CAPL
        spread_ids = jnp.arange(spread_slots, dtype=jnp.int32)
        spread_scores = jax.random.randint(fourth, (spread_slots,), 0, 1 << 20) * spread_slots + spread_ids
        spread_scores = jnp.where(spread_ids // CAPL == full_owner, spread_ids - spread_slots, spread_scores)
        spread_pick = jnp.argsort(spread_scores, stable=True)[:RL].astype(jnp.int32)
        owner_pick = spread_pick // CAPL
        spread_rows = SC * DEVICES + owner_pick * LC + jax.random.randint(fifth, (RL,), 0, LC)
        joined = jnp.concatenate([whole_rows, spread_rows]).astype(jnp.int32)
        shuffle = jax.random.permutation(sixth, ROWS_DEV)
        return joined[shuffle]
    return jax.vmap(one_block)(block_keys).reshape(-1).astype(jnp.int32)


def block_scale(own_key, extent, cuts, smallest, top_value):
    def one(dim, parts):
        steps = jax.random.uniform(jax.random.fold_in(jax.random.fold_in(own_key, 6), dim), (parts,), jnp.float32, smallest / len(cuts), top_value / len(cuts))
        return jnp.repeat(jnp.exp(steps), extent[dim] // parts).reshape((-1,) + (1,) * (len(extent) - dim - 1))

    factor_of = one(*cuts[0])
    for cut in cuts[1:]:
        factor_of = factor_of * one(*cut)
    return factor_of


def bell_draw(own_key, dims, scale, limit, cuts=(), kind=jnp.bfloat16):
    gain = block_scale(own_key, dims, cuts, -0.22, 0.18) if cuts else 1.0
    values = jax.random.normal(own_key, dims, jnp.float32) * scale * gain
    return jnp.minimum(jnp.maximum(values, -limit), limit).astype(kind)


def setup_inputs(seed: int = 0) -> dict:
    seeds = jax.random.split(jax.random.key(seed), 3)
    return {
        "embeddings": bell_draw(seeds[0], (ROWS, D), 1.0, 6.0, ((0, 512),)),
        "cluster_of": draw_cluster_of(jax.random.fold_in(seeds[2], 71), 0),
    }


kernel_scale = 32.0

def unit_norm(values):
    floats = values.astype(jnp.float32)
    scaled = floats * lax.rsqrt(lax.optimization_barrier(jnp.sum(floats * floats, axis=1, keepdims=True)) + 1e-06)
    return scaled.astype(jnp.bfloat16)

def reference(embeddings, cluster_of):
    unit_rows = unit_norm(embeddings)
    order = jnp.argsort(cluster_of, stable=True).astype(jnp.int32)
    sorted_rows = unit_rows[order]
    sorted_ids = cluster_of[order]
    margin = max(SS, N_SUB * LS)
    block_size = 512
    padded_rows = jnp.pad(sorted_rows, ((margin, margin), (0, 0)))
    padded_ids = jnp.pad(sorted_ids, (margin, margin), constant_values=-1)

    def one_block(block_index):
        block_start = (block_index * block_size).astype(jnp.int32)
        row_block = lax.dynamic_slice_in_dim(padded_rows, block_start + margin, block_size, 0)
        row_ids = lax.dynamic_slice_in_dim(padded_ids, block_start + margin, block_size, 0)
        window = lax.dynamic_slice_in_dim(padded_rows, block_start, block_size + 2 * margin, 0)
        window_ids = lax.dynamic_slice_in_dim(padded_ids, block_start, block_size + 2 * margin, 0)
        similar = jnp.dot(row_block, window.T, preferred_element_type=jnp.float32)
        row_place = block_start + margin + jnp.arange(block_size, dtype=jnp.int32)
        window_place = block_start + jnp.arange(block_size + 2 * margin, dtype=jnp.int32)
        same_cluster = row_ids[:, None] == window_ids[None, :]
        keep_pair = same_cluster & (row_place[:, None] != window_place[None, :])
        kernel_mass = lax.optimization_barrier(jnp.sum(jnp.where(keep_pair, jnp.exp(kernel_scale * similar), 0.0), axis=1))
        members = lax.optimization_barrier(jnp.sum(same_cluster.astype(jnp.float32), axis=1))
        return kernel_mass / members
    sorted_density = lax.map(one_block, jnp.arange(ROWS // block_size, dtype=jnp.int32)).reshape(-1)
    return jnp.zeros((ROWS,), jnp.float32).at[order].set(sorted_density)
```

```python
import functools

import jax
import jax.numpy as jnp
from jax import lax
from jax.experimental import pallas as pl
from jax.experimental.pallas import tpu as pltpu
from jax.sharding import PartitionSpec as P

MESH = pl.DeviceIdType.MESH
F32 = jnp.float32
BF16 = jnp.bfloat16
I32 = jnp.int32
NZ = 16
NY = 4
NS = 8
ND = NY * NS
MSG = 128
SCALE = 32.0


def iota(shape, axis):
    return lax.broadcasted_iota(I32, shape, axis)


def nn(left, right, precision=None):
    return lax.dot_general(
        left, right, (((1,), (0,)), ((), ())), precision=precision, preferred_element_type=F32
    )


def nt(left, right, precision=None):
    return lax.dot_general(
        left, right, (((1,), (1,)), ((), ())), precision=precision, preferred_element_type=F32
    )


def exact_nn(left, right):
    return nn(left, right, lax.Precision.HIGHEST)


def exact_nt(left, right):
    return nt(left, right, lax.Precision.HIGHEST)


def hot(condition, dtype=BF16):
    return jnp.where(condition, 1.0, 0.0).astype(dtype)


def step_of(message):
    place = message + 1
    return lax.rem(8 + (place // 2) * (2 * lax.rem(place, 2) - 1) + NZ, NZ)


def kernel(
    cap,
    x_ref,
    g_ref,
    tag_ref,
    v_ref,
    unit,
    send,
    recv,
    trecv,
    out_w,
    out_s,
    fin_w,
    fin_s,
    own,
    row_acc,
    col_acc,
    kinds,
    s_valid,
    back_a,
    got_a,
    back_b,
    got_b,
    z_send,
    z_recv,
    t_send,
    t_recv,
    w_send,
    w_recv,
    s_send,
    s_recv,
    a_sem,
    b_sem,
):
    dp = lax.axis_index("dp")
    sub = lax.axis_index("sub")
    z = dp // NY
    y = lax.rem(dp, NY)
    me = y * NS + sub

    def z_peer(step):
        return (lax.rem(z + step + NZ, NZ) * NY + y, sub)

    def plane_peer(d):
        return (z * NY + d // NS, lax.rem(d, NS))

    barrier = pltpu.get_barrier_semaphore()

    @pl.loop(1, NZ)
    def _(i):
        pl.semaphore_signal(barrier, inc=1, device_id=z_peer(i), device_id_type=MESH)

    @pl.loop(1, ND)
    def _(i):
        pl.semaphore_signal(
            barrier, inc=1, device_id=plane_peer(lax.rem(me + i, ND)), device_id_type=MESH
        )

    @pl.loop(0, 8)
    def _(i):
        rows = pl.ds(pl.multiple_of(i * 128, 128), 128)
        floats = x_ref[rows, :].astype(F32)
        total = jnp.sum(floats * floats, axis=1, keepdims=True)
        unit[rows, :] = (floats * lax.rsqrt(total + 1e-06)).astype(BF16)

    if cap < MSG:

        @pl.loop(0, NZ)
        def _(m):
            recv[m, cap:, :] = jnp.zeros((MSG - cap, 1024), BF16)

    pl.semaphore_wait(barrier, NZ - 1 + ND - 1)

    def z_copy(m):
        return pltpu.make_async_remote_copy(
            src_ref=send.at[m],
            dst_ref=recv.at[m, pl.ds(0, cap)],
            send_sem=z_send.at[m],
            recv_sem=z_recv.at[m],
            device_id=z_peer(step_of(m)),
            device_id_type=MESH,
        )

    def tag_copy(m):
        part = pl.ds(pl.multiple_of(m * 8, 8), 8)
        return pltpu.make_async_remote_copy(
            src_ref=tag_ref.at[part],
            dst_ref=trecv.at[part],
            send_sem=t_send.at[m],
            recv_sem=t_recv.at[m],
            device_id=z_peer(step_of(m)),
            device_id_type=MESH,
        )

    @pl.loop(0, NZ)
    def _(m):
        pick = hot(iota((cap, 1024), 0) + m * MSG == g_ref[...])
        rows = nn(pick, unit[...]).astype(BF16)

        @pl.when(m < NZ - 1)
        def _():
            send[m] = rows
            z_copy(m).start()
            tag_copy(m).start()

        @pl.when(m == NZ - 1)
        def _():
            recv[m, :cap, :] = rows
            trecv[(NZ - 1) * 8 :, :] = tag_ref[(NZ - 1) * 8 :, :]

    def part_of(d):
        return pl.ds(pl.multiple_of(d * 16, 16), 16)

    def w_copy(c, d):
        return pltpu.make_async_remote_copy(
            src_ref=out_w.at[c, part_of(d)],
            dst_ref=fin_w.at[c, part_of(me)],
            send_sem=w_send.at[c],
            recv_sem=w_recv.at[c],
            device_id=plane_peer(d),
            device_id_type=MESH,
        )

    def s_copy(c, d):
        return pltpu.make_async_remote_copy(
            src_ref=out_s.at[c, part_of(d // NS)],
            dst_ref=fin_s.at[c, part_of(me)],
            send_sem=s_send.at[c],
            recv_sem=s_recv.at[c],
            device_id=plane_peer(d),
            device_id_type=MESH,
        )

    def wait_all(ref, sem):
        pltpu.make_async_copy(ref, ref, sem).wait()

    def forward(c):
        for j in range(4):
            m = c * 4 + j

            @pl.when(m < NZ - 1)
            def _():
                z_copy(m).wait_recv()
                tag_copy(m).wait_recv()

        tags = trecv[pl.ds(pl.multiple_of(c * 32, 32), 32), :]
        tags = jnp.concatenate([tags[8 * j : 8 * j + 1] for j in range(4)], axis=1)
        value = tags.astype(I32) - 1
        lane = iota((1, 4 * MSG), 1)
        source = lane // MSG
        kind = (value & 1) + 1
        code = value >> 1
        rank = code & 3
        is_spread = code >= 4 * ND
        is_whole = (code >= 0) & (code < 4 * ND)
        w_dev = jnp.where(is_whole, code >> 2, -1)
        w_slot = source * 3 + rank
        s_dev = jnp.where(is_spread, (code >> 2) - ND, -1)
        s_slot = source * 4 + rank
        place = jnp.where(
            is_whole,
            w_dev * 16 + w_slot,
            jnp.where(is_spread, ND * 16 + s_dev * 16 + s_slot, -1),
        )
        pick = hot(iota((ND * 16 + NY * 16, 4 * MSG), 0) == place)
        w_kind = jnp.where(iota((ND, 4 * MSG), 0) == w_dev, kind, 0).astype(F32).astype(BF16)
        w_tags = nt(w_kind, hot(iota((128, 4 * MSG), 0) == w_slot))
        s_tags = nt(
            hot(iota((ND, 4 * MSG), 0) // NS == s_dev),
            hot(iota((128, 4 * MSG), 0) == s_slot),
        )
        line = iota((ND * 16, ND), 0)
        where_w = hot(line == iota((ND * 16, ND), 1) * 16 + 12)
        where_s = hot(line == iota((ND * 16, ND), 1) * 16 + 13)
        extra = nn(where_w, w_tags.astype(BF16)) + nn(where_s, s_tags.astype(BF16))
        rows = recv.at[pl.ds(c * 4, 4)]
        for n in range(4):
            cols = pl.ds(n * 256, 256)
            block = rows[:, :, cols].reshape(4 * MSG, 256)
            picked = nn(pick, block)
            whole = picked[: ND * 16]
            if n == 0:
                whole = jnp.concatenate([whole[:, :128] + extra, whole[:, 128:]], axis=1)
            out_w[c, :, cols] = whole.astype(BF16)
            out_s[c, :, cols] = picked[ND * 16 :].astype(BF16)

        @pl.loop(1, ND)
        def _(i):
            d = lax.rem(me + i, ND)
            w_copy(c, d).start()
            s_copy(c, d).start()

        fin_w[c, part_of(me), :] = out_w[c, part_of(me), :]
        fin_s[c, part_of(me), :] = out_s[c, part_of(y), :]

    def tags_of(c):
        line = iota((2 * ND, ND * 16), 1)
        head = iota((2 * ND, ND * 16), 0)
        want = jnp.where(head < ND, head * 16 + 12, (head - ND) * 16 + 13)
        return nn(hot(line == want), fin_w[c, :, 0:128])

    def as_rows(tags):
        line = iota((ND * 16, ND), 0)
        spread = nn(hot(line // 16 == iota((ND * 16, ND), 1)), tags.astype(BF16))
        keep = iota((ND * 16, 128), 1) == lax.rem(iota((ND * 16, 128), 0), 16)
        return jnp.sum(jnp.where(keep, spread, 0.0), axis=1, keepdims=True)

    def as_lanes(tags):
        spread = nn(
            tags.astype(BF16), hot(iota((128, ND * 16), 0) == lax.rem(iota((128, ND * 16), 1), 16))
        )
        keep = iota((ND, ND * 16), 0) == iota((ND, ND * 16), 1) // 16
        return jnp.sum(jnp.where(keep, spread, 0.0), axis=0, keepdims=True)

    def compute(c):
        wait_all(fin_w.at[c, pl.ds(0, (ND - 1) * 16)], w_recv.at[c])
        wait_all(fin_s.at[c, pl.ds(0, (ND - 1) * 16)], s_recv.at[c])
        tags = tags_of(c)
        w_tags = tags[:ND]
        kinds[:, pl.ds(0, 128)] += nn(
            w_tags.astype(BF16), hot(iota((128, 128), 1) == iota((128, 128), 0) + c * 16)
        )
        row_acc[c, :, 1:2] = as_rows(w_tags)
        s_valid[c, :, 0:1] = as_rows(tags[ND:])
        lanes = as_lanes(w_tags)
        lanes = jnp.where(lanes > 0.0, lanes, -1.0)
        right = fin_w[c]

        @pl.loop(0, c + 1)
        def _(b):
            similar = nt(fin_w[b], right)
            same = row_acc[b, :, 1:2] == lanes
            other = (iota((ND * 16, ND * 16), 0) != iota((ND * 16, ND * 16), 1)) | (b != c)
            weights = jnp.where(same & other, jnp.exp(SCALE * similar), 0.0)
            col_acc[c] += jnp.broadcast_to(
                jnp.sum(weights, axis=0, keepdims=True), (8, ND * 16)
            )

            @pl.when(b != c)
            def _():
                row_acc[b, :, 0:1] += jnp.sum(weights, axis=1, keepdims=True)

    kinds[...] = jnp.zeros_like(kinds)
    row_acc[...] = jnp.zeros_like(row_acc)
    col_acc[...] = jnp.zeros_like(col_acc)

    @pl.loop(0, 5)
    def _(c):
        @pl.when(c < 4)
        def _():
            forward(c)

        @pl.when(c > 0)
        def _():
            compute(c - 1)

    for c in range(4):
        for j in range(NY):
            own[c * 64 + j * 16 : c * 64 + j * 16 + 16, :] = fin_s[c, part_of(j * NS + sub), :]
    own_rows = own[...]
    lane = iota((1, 256), 1)
    own_chunk = lane // 64
    own_line = (lax.rem(lane, 64) // 16 * NS + sub) * 16 + lax.rem(lane, 16)
    s_mass = jnp.zeros((1, 256), F32)
    s_count = jnp.zeros((1, 1), F32)
    for c in range(4):
        similar = nt(fin_s[c], own_rows)
        valid = s_valid[c, :, 0:1]
        self_pair = (own_chunk == c) & (iota((ND * 16, 256), 0) == own_line)
        weights = jnp.where((valid > 0.0) & ~self_pair, jnp.exp(SCALE * similar), 0.0)
        s_mass += jnp.sum(weights, axis=0, keepdims=True)
        s_count += jnp.sum(valid, axis=0, keepdims=True)
    s_density = s_mass / jnp.maximum(s_count, 1.0)

    mass = jnp.zeros((ND, 128), F32)
    device_of = iota((ND, ND * 16), 1) // 16 == iota((ND, ND * 16), 0)
    for c in range(4):
        to_lane = iota((ND * 16, 128), 1) == c * 16 + lax.rem(iota((ND * 16, 128), 0), 16)
        placed = jnp.where(to_lane, row_acc[c, :, 0:1], 0.0)
        mass += jnp.sum(placed.reshape(ND, 16, 128), axis=1)
        masked = jnp.where(device_of, col_acc[c, 0:1, :], 0.0)
        mass += exact_nt(
            masked,
            hot(iota((128, ND * 16), 0) == c * 16 + lax.rem(iota((128, ND * 16), 1), 16), F32),
        )
    kind = kinds[...]
    first = jnp.sum(hot(kind == 1.0, F32), keepdims=True)
    second = jnp.sum(hot(kind == 2.0, F32), keepdims=True)
    density = jnp.where(
        kind > 0.0, mass / jnp.maximum(jnp.where(kind == 1.0, first, second), 1.0), 0.0
    )
    own_of = iota((ND, 256), 0) == lax.rem(iota((ND, 256), 1), 64) // 16 * NS + sub
    density += exact_nt(
        jnp.where(own_of, s_density, 0.0),
        hot(
            iota((128, 256), 0)
            == 64 + iota((128, 256), 1) // 64 * 16 + lax.rem(iota((128, 256), 1), 16),
            F32,
        ),
    )
    back_a[...] = exact_nn(hot(iota((ND * 8, ND), 0) // 8 == iota((ND * 8, ND), 1), F32), density)

    def lines_of(i):
        return pl.ds(pl.multiple_of(i * 8, 8), 8)

    @pl.loop(1, ND)
    def _(i):
        d = lax.rem(me + i, ND)
        pltpu.make_async_remote_copy(
            src_ref=back_a.at[lines_of(d)],
            dst_ref=got_a.at[lines_of(me)],
            send_sem=a_sem.at[0],
            recv_sem=a_sem.at[1],
            device_id=plane_peer(d),
            device_id_type=MESH,
        ).start()

    got_a[lines_of(me), :] = back_a[lines_of(me), :]
    wait_all(got_a.at[pl.ds(0, (ND - 1) * 8)], a_sem.at[1])
    lines = exact_nn(hot(iota((128, ND * 8), 1) == iota((128, ND * 8), 0) * 8, F32), got_a[...])
    head = iota((128, 128), 0)
    message = head // 8
    slot = lax.rem(head, 8)
    base = message // 4 * 16
    inner = lax.rem(message, 4)
    want = jnp.where(slot < 3, base + inner * 3 + slot, 64 + base + inner * 4 + slot - 3)
    want = jnp.where(slot < 7, want, -1)
    back_b[...] = exact_nt(hot(iota((128, 128), 1) == want, F32), lines)

    @pl.loop(0, NZ - 1)
    def _(m):
        pltpu.make_async_remote_copy(
            src_ref=back_b.at[lines_of(m)],
            dst_ref=got_b.at[lines_of(m)],
            send_sem=b_sem.at[0],
            recv_sem=b_sem.at[1],
            device_id=z_peer(NZ - step_of(m)),
            device_id_type=MESH,
        ).start()

    got_b[(NZ - 1) * 8 :, :] = back_b[(NZ - 1) * 8 :, :]
    wait_all(got_b.at[pl.ds(0, (NZ - 1) * 8)], b_sem.at[1])
    v_ref[...] = got_b[...]

    @pl.loop(0, NZ - 1)
    def _(m):
        z_copy(m).wait_send()
        tag_copy(m).wait_send()

    for c in range(4):
        wait_all(out_w.at[c, pl.ds(0, (ND - 1) * 16)], w_send.at[c])
        wait_all(fin_s.at[c, pl.ds(0, (ND - 1) * 16)], s_send.at[c])
    wait_all(back_a.at[pl.ds(0, (ND - 1) * 8)], a_sem.at[0])
    wait_all(back_b.at[pl.ds(0, (NZ - 1) * 8)], b_sem.at[0])


def exchange(cap, embeddings, spots, tags):
    vmem = pltpu.VMEM
    dma = pltpu.SemaphoreType.DMA
    return pl.pallas_call(
        functools.partial(kernel, cap),
        out_shape=jax.ShapeDtypeStruct((NZ * 8, 128), F32),
        in_specs=[pl.BlockSpec(memory_space=pltpu.VMEM)] * 3,
        out_specs=pl.BlockSpec(memory_space=pltpu.VMEM),
        scratch_shapes=[
            vmem((1024, 1024), BF16),
            vmem((NZ - 1, cap, 1024), BF16),
            vmem((NZ, MSG, 1024), BF16),
            vmem((NZ * 8, 128), F32),
            vmem((4, ND * 16, 1024), BF16),
            vmem((4, NY * 16, 1024), BF16),
            vmem((4, ND * 16, 1024), BF16),
            vmem((4, ND * 16, 1024), BF16),
            vmem((256, 1024), BF16),
            vmem((4, ND * 16, 128), F32),
            vmem((4, 8, ND * 16), F32),
            vmem((ND, 128), F32),
            vmem((4, ND * 16, 128), F32),
            vmem((ND * 8, 128), F32),
            vmem((ND * 8, 128), F32),
            vmem((NZ * 8, 128), F32),
            vmem((NZ * 8, 128), F32),
            dma((NZ,)),
            dma((NZ,)),
            dma((NZ,)),
            dma((NZ,)),
            dma((4,)),
            dma((4,)),
            dma((4,)),
            dma((4,)),
            dma((2,)),
            dma((2,)),
        ],
        compiler_params=pltpu.CompilerParams(
            collective_id=0, has_side_effects=True, vmem_limit_bytes=56 << 20
        ),
    )(embeddings, spots, tags)


def rank_within(labels):
    places = jnp.arange(labels.shape[0], dtype=I32)
    matches = (labels[:, None] == labels[None, :]) & (places[:, None] < places[None, :])
    return jnp.sum(matches.astype(I32), axis=0)


def local(embeddings, cluster_of):
    sub = lax.axis_index("sub")
    z = lax.axis_index("dp") // NY
    whole_count = 2 * NZ * ND
    whole = cluster_of < whole_count
    target = jnp.where(whole, cluster_of // 2, whole_count // 2 + cluster_of - whole_count)
    plane = jnp.where(whole, target // ND, (target - NZ * ND) // NY)
    rank = rank_within(target)
    spot = rank_within(plane)
    step = (plane - z + NZ) % NZ
    message = jnp.where(step >= 8, 2 * (step - 8), 2 * (8 - step) - 1)
    spots = message * MSG + spot
    device = jnp.where(whole, target % ND, (target - NZ * ND) % NY)
    code = jnp.where(whole, device * 4 + rank, 4 * ND + device * 4 + rank)
    value = 2 * code + jnp.where(whole, cluster_of % 2, 0) + 1
    slots = jnp.arange(NZ * MSG, dtype=I32)
    tags = jnp.sum(jnp.where(spots[None, :] == slots[:, None], value[None, :], 0), axis=1)
    tags = jnp.broadcast_to(tags.astype(F32).reshape(NZ, 1, MSG), (NZ, 8, MSG)).reshape(-1, MSG)
    cap = 112
    got = exchange(cap, embeddings, spots.reshape(1, -1), tags)
    line = message * 8 + jnp.where(whole, rank, 3 + rank)
    lane = jnp.where(whole, device, device * NS + sub)
    numbers = jnp.arange(128, dtype=I32)
    lines = nn(
        (line[:, None] == numbers[None, :]).astype(F32), got, lax.Precision.HIGHEST
    )
    return jnp.sum(jnp.where(lane[:, None] == numbers[None, :], lines, 0.0), axis=1)


def solution(mesh):
    placed = (P(("dp", "sub"), None), P(("dp", "sub")))
    return jax.shard_map(
        local, mesh=mesh, in_specs=placed, out_specs=P(("dp", "sub")), check_vma=False
    )
```
